32 devices in a mesh: atom: 4 (over y, x), pix: 8 (over z, core).
Axes of the slice: x: 2, y: 2, z: 4, core: 2. Of those that a mesh axis runs over, the one named last changes fastest.
Arguments:
- observed: float32 [224, 2048], P('atom', 'pix'), may hold values from -6 to 6
- library: float32 [224, 4096], P(None, ('atom', 'pix')), may hold values from -0.09375 to 0.09375
- image_split: float32 [224, 2048], P('atom', 'pix'), may hold values from -6 to 6
- image_dual: float32 [224, 2048], P('atom', 'pix'), may hold values from -4 to 4
- support: float32 [4096, 2048], P('atom', 'pix'), may hold values from -12 to 12
- support_dual: float32 [4096, 2048], P('atom', 'pix'), may hold values from -4 to 4
- positive: float32 [4096, 2048], P('atom', 'pix'), may hold values from 0 to 1
- positive_dual: float32 [4096, 2048], P('atom', 'pix'), may hold values from -4 to 4
Outputs:
- abundance: float32 [4096, 2048], P('atom', 'pix')
- image_split_next: float32 [224, 2048], P('atom', 'pix')
- image_dual_next: float32 [224, 2048], P('atom', 'pix')
- support_next: float32 [4096, 2048], P('atom', 'pix')
- support_dual_next: float32 [4096, 2048], P('atom', 'pix')
- positive_next: float32 [4096, 2048], P('atom', 'pix')
- positive_dual_next: float32 [4096, 2048], P('atom', 'pix')
The draws below stay inside these ranges and needn't reach their ends.
All inputs are finite; a program needn't handle non-finite values.
Results may differ from the reference program's by a relative error of at most 0.0001.
Values sent between devices are 32-bit elements; how exact they have to be, the bound alone decides.
No kernel may reach another device: no remote copies, remote signals or barrier semaphores. Data moves between devices by JAX's collectives and lax.ppermute only.
A program may use at most 64 MiB of HBM per device.

```python
import math
import jax
import jax.numpy as jnp
from jax import lax

BANDS = 224
ATOMS = 4096
ITERS = 4
NPIX = 2048


def draw_support(key, part):
    first_key, second_key = jax.random.split(jax.random.fold_in(key, 11))
    scales = jnp.exp(jax.random.uniform(first_key, (ATOMS, 1), jnp.float32, math.log(0.05), math.log(3.0)))
    base = jnp.clip(jax.random.normal(second_key, (ATOMS, NPIX), jnp.float32), -4.0, 4.0)
    return (scales * base).astype(jnp.float32)


def steps_of(own_key, extent, pieces, least, top_value):
    def one(position, parts):
        steps = jax.random.uniform(jax.random.fold_in(jax.random.fold_in(own_key, 6), position), (parts,), jnp.float32, least / len(pieces), top_value / len(pieces))
        return jnp.repeat(jnp.exp(steps), extent[position] // parts).reshape((-1,) + (1,) * (len(extent) - position - 1))

    factor_of = one(*pieces[0])
    for cut in pieces[1:]:
        factor_of = factor_of * one(*cut)
    return factor_of


def bell_draw(stream_key, extent, deviation, bound, pieces=(), kind=jnp.bfloat16):
    factor_of = steps_of(stream_key, extent, pieces, -0.22, 0.18) if pieces else 1.0
    array = jax.random.normal(stream_key, extent, jnp.float32) * deviation * factor_of
    return jnp.minimum(jnp.maximum(array, -bound), bound).astype(kind)


def setup_inputs(seed: int = 0) -> dict:
    splits = jax.random.split(jax.random.key(seed), 9)
    return {
        "observed": bell_draw(splits[0], (BANDS, NPIX), 1.0, 6.0, ((0, 4), (1, 8)), jnp.float32),
        "library": bell_draw(splits[1], (BANDS, ATOMS), ATOMS ** -0.5, 0.09375, ((1, 32),), jnp.float32),
        "image_split": bell_draw(splits[2], (BANDS, NPIX), 1.0, 6.0, ((0, 4), (1, 8)), jnp.float32),
        "image_dual": bell_draw(splits[3], (BANDS, NPIX), 0.3, 4.0, ((0, 4), (1, 8)), jnp.float32),
        "support": draw_support(jax.random.fold_in(splits[8], 71), 0),
        "support_dual": bell_draw(splits[5], (ATOMS, NPIX), 0.3, 4.0, ((0, 4), (1, 8)), jnp.float32),
        "positive": jnp.clip(1.0 * jax.random.uniform(splits[6], (ATOMS, NPIX), jnp.float32) ** steps_of(splits[6], (ATOMS, NPIX), ((0, 4), (1, 8)), -0.2, 0.2), 0.0, 1.0),
        "positive_dual": bell_draw(splits[7], (ATOMS, NPIX), 0.3, 4.0, ((0, 4), (1, 8)), jnp.float32),
    }


penalty = 0.5
shrink_rate = 0.4
epsilon = 1e-06

def matmul(left, right):
    return jnp.dot(left.astype(jnp.float32), right.astype(jnp.float32), precision=lax.Precision.HIGHEST, preferred_element_type=jnp.float32)

def reference(observed, library, image_split, image_dual, support, support_dual, positive, positive_dual):
    identity = jnp.eye(BANDS, dtype=jnp.float32)
    gram = matmul(library, library.T)
    inverse = jnp.linalg.solve(gram + 2.0 * identity, identity)
    level = shrink_rate * math.sqrt(NPIX)
    abundance = support
    for step in range(ITERS):
        right = matmul(library.T, image_split + image_dual) + support + support_dual + positive + positive_dual
        solved = matmul(inverse, matmul(library, right))
        abundance = 0.5 * (right - matmul(library.T, solved))
        mixed = matmul(library, abundance)
        image_split = (observed + penalty * (mixed - image_dual)) / (1.0 + penalty)
        image_dual = image_dual - (mixed - image_split)
        spread = abundance - support_dual
        squares = lax.optimization_barrier(jnp.sum(spread * spread, axis=1))
        support = spread * jnp.maximum(1.0 - level / jnp.sqrt(squares + epsilon), 0.0)[:, None]
        support_dual = support_dual - (abundance - support)
        positive = jnp.maximum(abundance - positive_dual, 0.0)
        positive_dual = positive_dual - (abundance - positive)
    return (abundance, image_split, image_dual, support, support_dual, positive, positive_dual)
```

```python
import functools
import math

import jax
import jax.numpy as jnp
from jax import lax
from jax.experimental import pallas as pl
from jax.experimental.pallas import tpu as pltpu
from jax.sharding import PartitionSpec as P

ITERS = 4

penalty = 0.5
shrink_rate = 0.4
epsilon = 1e-06
LANES = 128
NEWTON_CAP = 40
VMEM_LIMIT = 20 * 1024 * 1024

f32 = jnp.float32
bf16 = jnp.bfloat16
EXACT = lax.Precision.HIGHEST


def split(value):
    high = value.astype(bf16)
    return high, (value - high.astype(f32)).astype(bf16)


def dot(left, right, dims=((1,), (0,)), precision=None):
    return lax.dot_general(
        left, right, (dims, ((), ())), precision=precision, preferred_element_type=f32
    )


def dot3(left, right):
    (lh, ll), (rh, rl) = left, right
    return dot(lh, rh) + (dot(lh, rl) + dot(ll, rh))


def call(body, outs, scratch=(), name=None):
    return pl.pallas_call(
        body,
        out_shape=outs,
        scratch_shapes=list(scratch),
        compiler_params=pltpu.CompilerParams(vmem_limit_bytes=VMEM_LIMIT),
        name=name,
    )


def shape(*dims, dtype=f32):
    return jax.ShapeDtypeStruct(dims, dtype)


def packed_rows(bands):
    return bands if bands <= LANES else bands + (bands - LANES)


def gram_body(block_ref, packed_ref):
    bands = block_ref.shape[0]
    block = block_ref[...]
    gram = dot(block, block, ((1,), (1,)), EXACT)
    if bands <= LANES:
        packed_ref[...] = gram
        return
    packed_ref[:bands, :] = gram[:, :LANES]
    packed_ref[bands:, :] = jnp.zeros((bands - LANES, LANES), f32)
    packed_ref[bands:, : bands - LANES] = gram[LANES:, LANES:]


def transpose_body(block_ref, high_ref, low_ref):
    bands, atoms = block_ref.shape
    for first in range(0, atoms, LANES):
        high, low = split(block_ref[:, first : first + LANES].T)
        high_ref[first : first + LANES, :] = high
        low_ref[first : first + LANES, :] = low


def start_body(
    own_first, block_ref, image_ref, dual_ref, a_ref, b_ref, c_ref, d_ref, sum_ref, right_ref
):
    own = image_ref.shape[0]

    @pl.when(pl.program_id(0) == 0)
    def _():
        right_ref[...] = jnp.zeros_like(right_ref)
        first = pl.multiple_of(own_first[0], 8)
        right_ref[pl.ds(first, own), :] = 2.0 * (image_ref[...] + dual_ref[...])

    total = (a_ref[...] + b_ref[...]) + (c_ref[...] + d_ref[...])
    sum_ref[...] = total
    right_ref[...] -= dot(block_ref[...], total, precision=EXACT)


def start(own_first, block, image, dual, a, b, c, d):
    bands, atoms = block.shape
    own, pixels = image.shape
    rows = min(atoms, 256)
    wide = pl.BlockSpec((rows, pixels), lambda i, _: (i, 0))
    whole = pl.BlockSpec((own, pixels), lambda i, _: (0, 0))
    return pl.pallas_call(
        start_body,
        out_shape=(shape(atoms, pixels), shape(bands, pixels)),
        grid_spec=pltpu.PrefetchScalarGridSpec(
            num_scalar_prefetch=1,
            grid=(atoms // rows,),
            in_specs=[pl.BlockSpec((bands, rows), lambda i, _: (0, i)), whole, whole]
            + [wide] * 4,
            out_specs=(wide, pl.BlockSpec((bands, pixels), lambda i, _: (0, 0))),
        ),
        compiler_params=pltpu.CompilerParams(
            vmem_limit_bytes=VMEM_LIMIT, dimension_semantics=("arbitrary",)
        ),
        name="start",
    )(own_first, block, image, dual, a, b, c, d)


def inverse_body(one_ref, two_ref, inverse_ref, matrix_ref, residual_ref):
    bands = inverse_ref.shape[0]
    rows = lax.broadcasted_iota(jnp.int32, (bands, bands), 0)
    columns = lax.broadcasted_iota(jnp.int32, (bands, bands), 1)
    identity = jnp.where(rows == columns, 1.0, 0.0).astype(f32)
    packed = one_ref[...] + two_ref[...]
    if bands <= LANES:
        matrix_ref[...] = packed
    else:
        rest = bands - LANES
        matrix_ref[:, :LANES] = packed[:bands]
        matrix_ref[:LANES, LANES:] = packed[LANES:bands].T
        matrix_ref[LANES:, LANES:] = packed[bands:, :rest]
    matrix = matrix_ref[...] + 2.0 * identity
    matrix_ref[...] = matrix
    bound = jnp.max(jnp.sum(jnp.abs(matrix), axis=0))
    first = 2.0 / (2.0 + bound)
    residual = identity - first * matrix
    inverse_ref[...] = first * (identity + residual)

    def measure():
        residual_ref[...] = identity - dot(matrix_ref[...], inverse_ref[...], precision=EXACT)
        return jnp.max(jnp.sum(jnp.abs(residual_ref[...]), axis=0))

    def unfinished(state):
        step, size = state
        return jnp.logical_and(step < NEWTON_CAP, size > 1e-3)

    def improve():
        held = inverse_ref[...]
        inverse_ref[...] = held + dot(held, residual_ref[...], precision=EXACT)

    def again(state):
        step, _ = state
        improve()
        return step + 1, measure()

    lax.while_loop(unfinished, again, (jnp.int32(0), measure()))
    improve()


def factor_body(own_first, inverse_ref, block_ref, th_ref, tl_ref, eh_ref, el_ref):
    own = eh_ref.shape[1]
    inverse = inverse_ref[...]
    halves = split(inverse)
    atoms = block_ref.shape[1]
    step = min(atoms, 256)
    for first in range(0, atoms, step):
        high, low = split(dot3(halves, split(block_ref[:, first : first + step])))
        th_ref[:, first : first + step] = high
        tl_ref[:, first : first + step] = low
    mine = inverse_ref[pl.ds(pl.multiple_of(own_first[0], 8), own), :]
    high, low = split(2.0 * mine.T)
    eh_ref[...] = high
    el_ref[...] = low


def row_sums(squared, out_ref, index):
    pixels = squared.shape[1]
    folded = squared[:, :LANES]
    for first in range(LANES, pixels, LANES):
        folded = folded + squared[:, first : first + LANES]
    out_ref[index : index + 1, :] = jnp.sum(folded.T, axis=0, keepdims=True)


def image_step(own_first, u_ref, observed_ref, image_ref, dual_ref, image_out, dual_out):
    own = image_ref.shape[0]
    u = u_ref[pl.ds(pl.multiple_of(own_first[0], 8), own), :]
    image = image_ref[...]
    new = (2.0 * observed_ref[...] + image - u) / 3.0
    image_out[...] = new
    dual_out[...] = new - image + u


def first_body(
    own_first, one, two, inverse, lth, ltl, total, support_dual, positive_dual,
    observed, image, dual, spread, q, squares, image_out, dual_out, u_ref,
):
    u_ref[...] = dot(inverse[...], one[...] + two[...], precision=EXACT)
    halves = split(u_ref[...])
    atoms = spread.shape[0]
    for index in range(atoms // LANES):
        rows = slice(index * LANES, (index + 1) * LANES)
        y = dot3((lth[rows, :], ltl[rows, :]), halves)
        x = 0.5 * (total[rows, :] + y)
        new = x - support_dual[rows, :]
        spread[rows, :] = new
        q[rows, :] = x - positive_dual[rows, :]
        row_sums(new * new, squares, index)
    image_step(own_first, u_ref, observed, image, dual, image_out, dual_out)


def middle_body(
    own_first, one, two, lth, ltl, spread, q, w, observed, image, dual,
    spread_out, q_out, squares, image_out, dual_out, u_ref,
):
    u_ref[...] = one[...] + two[...]
    halves = split(u_ref[...])
    atoms = spread.shape[0]
    for index in range(atoms // LANES):
        rows = slice(index * LANES, (index + 1) * LANES)
        y = dot3((lth[rows, :], ltl[rows, :]), halves)
        old = q[rows, :]
        new = 0.5 * (spread[rows, :] + jnp.abs(old) + y)
        spread_out[rows, :] = new
        q_out[rows, :] = 0.5 * (w[rows, :] + old + y)
        row_sums(new * new, squares, index)
    image_step(own_first, u_ref, observed, image, dual, image_out, dual_out)


def last_body(
    own_first, one, two, lth, ltl, spread, q, w, observed, image, dual,
    spread_out, x_out, positive_out, positive_dual_out, squares, image_out, dual_out, u_ref,
):
    u_ref[...] = one[...] + two[...]
    halves = split(u_ref[...])
    atoms = spread.shape[0]
    for index in range(atoms // LANES):
        rows = slice(index * LANES, (index + 1) * LANES)
        y = dot3((lth[rows, :], ltl[rows, :]), halves)
        old = q[rows, :]
        new = 0.5 * (spread[rows, :] + jnp.abs(old) + y)
        spread_out[rows, :] = new
        row_sums(new * new, squares, index)
        newer = 0.5 * (w[rows, :] + old + y)
        x_out[rows, :] = newer + jnp.maximum(-old, 0.0)
        positive_out[rows, :] = jnp.maximum(newer, 0.0)
        positive_dual_out[rows, :] = jnp.maximum(-newer, 0.0)
    image_step(own_first, u_ref, observed, image, dual, image_out, dual_out)


def shrink_of(parts, level):
    squares = jnp.sum(parts[...], axis=0)
    return jnp.maximum(1.0 - level / jnp.sqrt(squares + epsilon), 0.0)


def column(row, pixels):
    turned = jnp.broadcast_to(row, (LANES, LANES)).T
    return jnp.concatenate([turned] * (pixels // LANES), axis=1)


def shrink_body(level, parts, spread, q, th, tl, eh, el, image, dual, w, right, hh, hl):
    gain = 2.0 * shrink_of(parts, level) - 1.0
    atoms, pixels = spread.shape
    for index in range(atoms // LANES):
        rows = slice(index * LANES, (index + 1) * LANES)
        scaled = column(gain[index : index + 1, :], pixels) * spread[rows, :]
        w[rows, :] = scaled
        high, low = split(scaled + jnp.abs(q[rows, :]))
        hh[rows, :] = high
        hl[rows, :] = low
    combined = split(image[...] + dual[...])
    right[...] = dot3((eh[...], el[...]), combined) - dot3(
        (th[...], tl[...]), (hh[...], hl[...])
    )


def end_body(level, parts, spread, support_out, dual_out):
    shrink = shrink_of(parts, level)
    atoms, pixels = spread.shape
    for index in range(atoms // LANES):
        rows = slice(index * LANES, (index + 1) * LANES)
        held = spread[rows, :]
        support = column(shrink[index : index + 1, :], pixels) * held
        support_out[rows, :] = support
        dual_out[rows, :] = support - held


def over_atoms(value):
    size = lax.axis_size("atom")
    if size == 1 or size & (size - 1):
        return lax.psum(value, "atom"), jnp.zeros_like(value)
    step = 1
    while True:
        other = lax.ppermute(value, "atom", [(i, i ^ step) for i in range(size)])
        step *= 2
        if step == size:
            return value, other
        value = value + other


def over_pixels(value):
    size = lax.axis_size("pix")
    copies = jnp.broadcast_to(value[None], (size,) + value.shape)
    return lax.all_to_all(copies, "pix", 0, 0, tiled=True)


def on_device(
    observed, library, image_split, image_dual, support, support_dual, positive, positive_dual
):
    block = lax.all_gather(library, "pix", axis=1, tiled=True)
    bands, atoms = block.shape
    own, pixels = image_split.shape
    level = shrink_rate * math.sqrt(lax.axis_size("pix") * pixels)
    own_first = (lax.axis_index("atom") * own).astype(jnp.int32).reshape(1)

    smem = pl.BlockSpec(memory_space=pltpu.SMEM)
    vmem = pl.BlockSpec(memory_space=pltpu.VMEM)

    def placed(body, outs, count, scratch, name):
        return pl.pallas_call(
            body,
            out_shape=outs,
            in_specs=[smem] + [vmem] * (count - 1),
            out_specs=tuple(vmem for _ in outs),
            scratch_shapes=list(scratch),
            compiler_params=pltpu.CompilerParams(vmem_limit_bytes=VMEM_LIMIT),
            name=name,
        )

    packed = call(gram_body, shape(packed_rows(bands), min(bands, LANES)), name="gram")(block)
    gram_one, gram_two = over_atoms(packed)
    total, right = start(
        own_first, block, image_split, image_dual, support, support_dual, positive, positive_dual
    )
    right_one, right_two = over_atoms(right)
    half = shape(atoms, bands, dtype=bf16)
    lth, ltl = call(transpose_body, (half, half), name="turn")(block)
    inverse = call(
        inverse_body,
        shape(bands, bands),
        [pltpu.VMEM((bands, bands), f32), pltpu.VMEM((bands, bands), f32)],
        name="inverse",
    )(gram_one, gram_two)
    half = shape(bands, atoms, dtype=bf16)
    edge = shape(bands, own, dtype=bf16)
    th, tl, eh, el = placed(factor_body, (half, half, edge, edge), 3, (), "factor")(
        own_first, inverse, block
    )

    wide = shape(atoms, pixels)
    band = shape(own, pixels)
    sums = shape(atoms // LANES, LANES)
    u_scratch = pltpu.VMEM((bands, pixels), f32)
    spread, q, squares, image, dual = placed(
        first_body, (wide, wide, sums, band, band), 12, [u_scratch], "first"
    )(
        own_first, right_one, right_two, inverse, lth, ltl, total, support_dual, positive_dual,
        observed, image_split, image_dual,
    )
    for step in range(1, ITERS):
        w, right = call(
            functools.partial(shrink_body, level),
            (wide, shape(bands, pixels)),
            [pltpu.VMEM((atoms, pixels), bf16), pltpu.VMEM((atoms, pixels), bf16)],
            name="shrink",
        )(over_pixels(squares), spread, q, th, tl, eh, el, image, dual)
        one, two = over_atoms(right)
        operands = (own_first, one, two, lth, ltl, spread, q, w, observed, image, dual)
        if step < ITERS - 1:
            spread, q, squares, image, dual = placed(
                middle_body, (wide, wide, sums, band, band), 11, [u_scratch], "middle"
            )(*operands)
        else:
            spread, x, pos, pos_dual, squares, image, dual = placed(
                last_body, (wide, wide, wide, wide, sums, band, band), 11, [u_scratch], "last"
            )(*operands)
    new_support, new_support_dual = call(
        functools.partial(end_body, level), (wide, wide), name="end"
    )(over_pixels(squares), spread)
    return (x, image, dual, new_support, new_support_dual, pos, pos_dual)


def solution(mesh):
    wide = P("atom", "pix")
    in_specs = (wide, P(None, ("atom", "pix"))) + (wide,) * 6
    return jax.shard_map(
        on_device, mesh=mesh, in_specs=in_specs, out_specs=(wide,) * 7, check_vma=False
    )
```
